32 devices in a mesh: groups: 1, lat: 16 (over z, y, x), lon: 2 (over core).
Axes of the slice: x: 2, y: 2, z: 4, core: 2. Of those that a mesh axis runs over, the one named last changes fastest.
Arguments:
- fields: bfloat16 [64, 128, 256], P('groups', 'lat', 'lon'), may hold values from -6 to 6
- conv_first: bfloat16 [64, 64, 3, 3], replicated, may hold values from -0.25 to 0.25
- conv_second: bfloat16 [64, 64, 3, 3], replicated, may hold values from -0.25 to 0.25
- mixing: bfloat16 [64, 64, 64], P(None, 'lon'), may hold values from -0.75 to 0.75
Outputs:
- result: bfloat16 [64, 128, 256], P(('groups', 'lon'), 'lat')
The draws below stay inside these ranges and needn't reach their ends.
All inputs are finite; a program needn't handle non-finite values.
Results may differ from the reference program's by a relative error of at most 0.0095.
Values may be sent and summed in bfloat16 or wider, within the bound.
A program may use at most 64 MiB of HBM per device.

```python
import math
import jax
import jax.numpy as jnp
from jax import lax

C = 64
NLAT = 128
NLON = 256
MMAX = 64
LDEG = 64
N_LAT = 16


def steps_of(key, dims, split, smallest, largest):
    def one(axis_at, blocks):
        draws = jax.random.uniform(jax.random.fold_in(jax.random.fold_in(key, 6), axis_at), (blocks,), jnp.float32, smallest / len(split), largest / len(split))
        return jnp.repeat(jnp.exp(draws), dims[axis_at] // blocks).reshape((-1,) + (1,) * (len(dims) - axis_at - 1))

    factor_of = one(*split[0])
    for cut in split[1:]:
        factor_of = factor_of * one(*cut)
    return factor_of


def centred(stream_key, shape, deviation, limit, shards=(), held_as=jnp.bfloat16):
    values = jax.random.normal(stream_key, shape, jnp.float32) * deviation
    if len(shards) > 0:
        values = steps_of(stream_key, shape, shards, -0.22, 0.18) * values
    return jnp.clip(values, min=-limit, max=limit).astype(held_as)


def setup_inputs(seed: int = 0, part: int = 0) -> dict:
    splits = jax.random.split(jax.random.key(seed), 5)
    own_keys = jax.random.split(jax.random.fold_in(splits[4], part), 5)
    fields = centred(own_keys[0], (C, NLAT, NLON), 1.0, 6.0, ((1, 16), (2, 2)))
    conv_first = centred(splits[1], (C, C, 3, 3), (9 * C) ** -0.5, 0.25)
    conv_second = centred(splits[2], (C, C, 3, 3), (9 * C) ** -0.5, 0.25)
    mixing = centred(splits[3], (LDEG, C, C), C ** -0.5, 0.75, ((1, 2),))
    return {"fields": fields, "conv_first": conv_first, "conv_second": conv_second, "mixing": mixing}


def forward_table(lon_total, orders):
    points = jnp.arange(lon_total, dtype=jnp.int32)[:, None]
    waves = jnp.arange(orders, dtype=jnp.int32)[None, :]
    angle = (points * waves % lon_total).astype(jnp.float32) * (2.0 * math.pi / lon_total)
    stacked = jnp.stack([jnp.cos(angle), -jnp.sin(angle)], axis=-1)
    return stacked.reshape(lon_total, 2 * orders).astype(jnp.bfloat16)

def inverse_table(lon_total, orders):
    waves = jnp.arange(orders, dtype=jnp.int32)[:, None]
    points = jnp.arange(lon_total, dtype=jnp.int32)[None, :]
    angle = (points * waves % lon_total).astype(jnp.float32) * (2.0 * math.pi / lon_total)
    factor = jnp.where(waves == 0, 1.0, 2.0).astype(jnp.float32)
    stacked = jnp.stack([factor * jnp.cos(angle), -factor * jnp.sin(angle)], axis=1)
    return stacked.reshape(2 * orders, lon_total).astype(jnp.bfloat16)

def quadrature(lat_total, lon_total):
    lat_rows = jnp.arange(lat_total, dtype=jnp.int32).astype(jnp.float32)
    colatitude = (lat_rows + 0.5) * (math.pi / lat_total)
    return jnp.sin(colatitude) * (math.pi / lat_total / lon_total)

def legendre_table(order_ids, degrees, lat_total):
    half_rows = lat_total // 2
    lat_rows = jnp.arange(half_rows, dtype=jnp.int32).astype(jnp.float32)
    colatitude = (lat_rows + 0.5) * (math.pi / lat_total)
    cosine = jnp.cos(colatitude)[None, :]
    sine_theta = jnp.sin(colatitude)[None, :]
    orders = order_ids.astype(jnp.float32)[:, None]
    counter = jnp.arange(1, degrees + 1, dtype=jnp.int32).astype(jnp.float32)
    log_terms = jnp.log((2.0 * counter - 1.0) / (2.0 * counter))
    below = counter[None, :] <= orders
    log_start = 0.5 * jnp.log(orders + 0.5) + 0.5 * lax.optimization_barrier(jnp.sum(jnp.where(below, log_terms[None, :], 0.0), axis=1, keepdims=True))
    log_start = log_start + orders * jnp.log(sine_theta)
    block_span = 32 if degrees % 32 == 0 else degrees

    def advance(carry, block_index):
        current, previous, log_scale = carry
        emitted = []
        for offset in range(block_span):
            degree = (block_index * block_span + offset).astype(jnp.float32)
            earlier = degree - 1.0
            coef_a = jnp.sqrt(jnp.maximum(4.0 * degree * degree - 1.0, 1.0) / jnp.maximum(degree * degree - orders * orders, 1.0))
            coef_b = jnp.sqrt(jnp.maximum(earlier * earlier - orders * orders, 0.0) / jnp.maximum(4.0 * earlier * earlier - 1.0, 1.0))
            newest = coef_a * (cosine * current - coef_b * previous)
            is_start = degree == orders
            before = degree < orders
            newest = jnp.where(before, 0.0, jnp.where(is_start, 1.0, newest))
            log_scale = jnp.where(is_start, log_start, log_scale)
            previous = jnp.where(is_start | before, 0.0, current)
            current = newest
            emitted.append(newest * jnp.exp(log_scale))
        size_now = jnp.maximum(jnp.abs(current), jnp.abs(previous))
        safe_size = jnp.where(size_now > 0.0, size_now, 1.0)
        carry_out = (current / safe_size, previous / safe_size, log_scale + jnp.log(safe_size))
        return (carry_out, jnp.stack(emitted, axis=-1))
    zeros = jnp.zeros((order_ids.shape[0], half_rows), jnp.float32)
    blocks = jnp.arange(degrees // block_span, dtype=jnp.int32)
    unused, stacked = lax.scan(advance, (zeros, zeros, zeros), blocks)
    northern = jnp.transpose(stacked, (1, 2, 0, 3)).reshape(order_ids.shape[0], half_rows, degrees)
    degree_ids = jnp.arange(degrees, dtype=jnp.int32)
    parity = (1 - 2 * ((degree_ids[None, :] + order_ids[:, None]) % 2)).astype(jnp.float32)
    southern = northern[:, ::-1, :] * parity[:, None, :]
    return jnp.concatenate([northern, southern], axis=1).astype(jnp.bfloat16)

def conv_layer(values, kernel):
    padded = jnp.pad(values, ((0, 0), (1, 1), (0, 0)))
    padded = jnp.concatenate([padded[:, :, -1:], padded, padded[:, :, :1]], axis=2)
    result = lax.conv_general_dilated(padded[None].astype(jnp.float32), kernel.astype(jnp.float32), (1, 1), 'VALID', dimension_numbers=('NCHW', 'OIHW', 'NCHW'), precision=lax.Precision.HIGHEST)[0]
    return jnp.maximum(result, 0.0).astype(jnp.bfloat16)

def reference(fields, conv_first, conv_second, mixing):
    hidden = conv_layer(conv_layer(fields, conv_first), conv_second)
    lat_total = NLAT
    lon_total = NLON
    orders = MMAX
    spectra = jnp.dot(hidden.reshape(C * lat_total, lon_total), forward_table(lon_total, orders), preferred_element_type=jnp.float32)
    spectra = spectra.reshape(C, lat_total, 2 * orders)
    coeffs = (spectra * quadrature(lat_total, lon_total)[None, :, None]).astype(jnp.bfloat16)
    per_group = orders // N_LAT
    pieces = jnp.moveaxis(coeffs.reshape(C, lat_total, N_LAT, per_group, 2), 2, 0)

    def one_group(inputs):
        group_index, item_block = inputs
        order_ids = (group_index * per_group + jnp.arange(per_group, dtype=jnp.int32)).astype(jnp.int32)
        legendre = legendre_table(order_ids, LDEG, lat_total).astype(jnp.float32)
        spectral = jnp.einsum('cjmr,mjl->lcmr', item_block.astype(jnp.float32), legendre).astype(jnp.bfloat16)
        mixed_coef = jnp.einsum('lcmr,loc->lomr', spectral.astype(jnp.float32), mixing.astype(jnp.float32)).astype(jnp.bfloat16)
        return jnp.einsum('lomr,mjl->ojmr', mixed_coef.astype(jnp.float32), legendre).astype(jnp.bfloat16)
    synthesis = lax.map(one_group, (jnp.arange(N_LAT, dtype=jnp.int32), pieces))
    synthesis = jnp.moveaxis(synthesis, 0, 2).reshape(C * lat_total, 2 * orders)
    result = jnp.dot(synthesis, inverse_table(lon_total, orders), preferred_element_type=jnp.float32)
    return result.reshape(C, lat_total, lon_total).astype(jnp.bfloat16)
```

```python
import functools
import math

import jax
import jax.numpy as jnp
import numpy as np
from jax import lax
from jax.experimental import pallas as pl
from jax.experimental.pallas import tpu as pltpu
from jax.sharding import PartitionSpec as P

MESH = pl.DeviceIdType.MESH
BF16 = jnp.bfloat16
F32 = jnp.float32


def mm(a, b, dims=((1,), (0,))):
    return lax.dot_general(a, b, (dims, ((), ())), preferred_element_type=F32)


def constant_tables(lat_count, rows, lon_total, orders, width, chans):
    lat_total = lat_count * rows
    per_x = 2 * orders // lat_count
    bf = jnp.bfloat16.dtype if hasattr(jnp.bfloat16, "dtype") else jnp.bfloat16
    k = np.arange(lon_total)[:, None]
    m = np.arange(orders)[None, :]
    angle = (k * m % lon_total).astype(np.float64) * (2.0 * math.pi / lon_total)
    forward = np.stack([np.cos(angle), -np.sin(angle)], axis=-1).reshape(lon_total, 2 * orders)
    factor = np.where(np.arange(orders) == 0, 1.0, 2.0)[:, None, None]
    inverse = np.stack([np.cos(angle.T), -np.sin(angle.T)], axis=1) * factor
    inverse = inverse.reshape(2 * orders, lon_total)
    forward = forward.T.reshape(lat_count, per_x, lon_total).transpose(1, 0, 2)
    forward = forward.reshape(2 * orders, lon_total)
    theta = (np.arange(lat_total) + 0.5) * (math.pi / lat_total)
    quad = np.sin(theta) * (math.pi / lat_total / lon_total)
    quad = np.broadcast_to(quad.reshape(lat_count, rows, 1), (lat_count, rows, width))
    half = lat_total // 2
    fold = np.concatenate([np.arange(half), np.arange(half)[::-1]])
    cosine = np.cos(theta[fold])[None, :]
    counter = np.arange(1, orders + 1)
    sums = np.concatenate([[0.0], np.cumsum(np.log((2.0 * counter - 1.0) / (2.0 * counter)))])
    ids = np.arange(orders)
    start = (0.5 * np.log(ids + 0.5) + 0.5 * sums[ids])[:, None] + ids[:, None] * np.log(np.sin(theta[fold]))[None, :]
    start = start.reshape(lat_count, per_x // 2, lat_total)
    pick = np.arange(lat_count)[:, None] == (np.arange(lat_total) // rows)[None, :]
    lane = np.arange(width) % chans
    squeeze = np.concatenate(
        [(lane[:, None] + h * chans) == np.arange(2 * chans)[None, :] for h in range(2)], axis=0
    )
    spread = lane[:, None] == lane[None, :]
    as_bf = lambda a: jnp.asarray(np.asarray(a, np.float32).astype(bf))
    as_f = lambda a: jnp.asarray(np.ascontiguousarray(a, np.float32))
    return (
        as_bf(forward), as_bf(inverse), as_f(quad), as_f(cosine), as_f(start),
        as_bf(pick), as_bf(squeeze), as_bf(spread),
    )


def body(sizes, x_ref, w1_ref, w2_ref, mix_ref, fwd_ref, inv_ref, quad_ref, cos_ref, start_ref,
         pick_ref, sq_ref, sp_ref, out_ref,
         xin, slab1, slab2, hdup, tb, send_b, recv_b, lt, lg, spec, tc, send_c, recv_c, mixed,
         a_send, a_recv, b_send, b_recv, c_send, c_recv):
    np_, rows, chans, half_w, degrees = sizes
    ch = chans // 2
    width = 2 * half_w
    per_x = 8
    orders_here = per_x // 2
    lat_total = np_ * rows
    lane_w = per_x * ch
    me = lax.axis_index("lat")
    core = lax.axis_index("lon")
    other = 1 - core

    barrier = pltpu.get_barrier_semaphore()

    def greet(d, _):
        p = lax.rem(me + d, np_)
        for h in range(2):
            pl.semaphore_signal(
                barrier, inc=1, device_id={"lat": p, "lon": (core + h) % 2}, device_id_type=MESH
            )
        return 0

    pl.semaphore_signal(barrier, inc=1, device_id={"lat": me, "lon": other}, device_id_type=MESH)
    lax.fori_loop(1, np_, greet, 0)

    cosine = cos_ref[...]
    log_start = start_ref[me]
    order = (me * orders_here + lax.broadcasted_iota(jnp.int32, (orders_here, lat_total), 0)).astype(F32)
    southern = lax.broadcasted_iota(jnp.int32, (orders_here, lat_total), 1) >= lat_total // 2
    order_odd = lax.broadcasted_iota(jnp.int32, (orders_here, lat_total), 0) + me * orders_here
    span = 32 if degrees % 32 == 0 else degrees

    def advance(block, carry):
        current, previous, log_scale = carry
        for offset in range(span):
            l_id = block * span + offset
            degree = l_id.astype(F32)
            earlier = degree - 1.0
            coef_a = jnp.sqrt(
                jnp.maximum(4.0 * degree * degree - 1.0, 1.0) / jnp.maximum(degree * degree - order * order, 1.0)
            )
            coef_b = jnp.sqrt(
                jnp.maximum(earlier * earlier - order * order, 0.0) / jnp.maximum(4.0 * earlier * earlier - 1.0, 1.0)
            )
            newest = coef_a * (cosine * current - coef_b * previous)
            is_start = order == degree
            before = order > degree
            newest = jnp.where(before, 0.0, jnp.where(is_start, 1.0, newest))
            log_scale = jnp.where(is_start, log_start, log_scale)
            previous = jnp.where(is_start | before, 0.0, current)
            current = newest
            value = newest * jnp.exp(log_scale)
            flip = southern & (((order_odd + l_id) & 1) == 1)
            value = jnp.where(flip, -value, value)
            for q in range(orders_here):
                lt[pl.ds(q * degrees + l_id, 1), :] = value[q : q + 1, :]
        size_now = jnp.maximum(jnp.abs(current), jnp.abs(previous))
        safe = jnp.where(size_now > 0.0, size_now, 1.0)
        return (current / safe, previous / safe, log_scale + jnp.log(safe))

    zeros = jnp.zeros((orders_here, lat_total), F32)
    lax.fori_loop(0, degrees // span, advance, (zeros, zeros, zeros))
    for q in range(orders_here):
        lg[q] = lt[q * degrees : (q + 1) * degrees, :].T.astype(BF16)

    pl.semaphore_wait(barrier, 2 * np_ - 1)

    def across():
        return pltpu.make_async_remote_copy(
            src_ref=x_ref, dst_ref=xin.at[core, pl.ds(2, rows)],
            send_sem=a_send.at[4], recv_sem=a_recv.at[4],
            device_id={"lat": me, "lon": other}, device_id_type=MESH,
        )

    def up(h):
        return pltpu.make_async_remote_copy(
            src_ref=x_ref.at[pl.ds(0, 2)], dst_ref=xin.at[core, pl.ds(rows + 2, 2)],
            send_sem=a_send.at[h], recv_sem=a_recv.at[h],
            device_id={"lat": jnp.maximum(me - 1, 0), "lon": (core + h) % 2}, device_id_type=MESH,
        )

    def down(h):
        return pltpu.make_async_remote_copy(
            src_ref=x_ref.at[pl.ds(rows - 2, 2)], dst_ref=xin.at[core, pl.ds(0, 2)],
            send_sem=a_send.at[2 + h], recv_sem=a_recv.at[2 + h],
            device_id={"lat": jnp.minimum(me + 1, np_ - 1), "lon": (core + h) % 2}, device_id_type=MESH,
        )

    @pl.when(me > 0)
    def _():
        up(0).start()
        up(1).start()

    @pl.when(me < np_ - 1)
    def _():
        down(0).start()
        down(1).start()

    across().start()

    @pl.when(me == 0)
    def _():
        xin[:, pl.ds(0, 2)] = jnp.zeros((2, 2, chans, half_w), BF16)

    @pl.when(me == np_ - 1)
    def _():
        xin[:, pl.ds(rows + 2, 2)] = jnp.zeros((2, 2, chans, half_w), BF16)

    xin[core, pl.ds(2, rows)] = x_ref[...]
    across().wait()

    def fill(slab, t, wide):
        base = t * 3 * chans
        slab[base : base + chans, :] = pltpu.roll(wide, 1, 1).astype(BF16)
        slab[base + chans : base + 2 * chans, :] = wide.astype(BF16)
        slab[base + 2 * chans : base + 3 * chans, :] = pltpu.roll(wide, width - 1, 1).astype(BF16)

    def row_in(t):
        return jnp.concatenate([xin[0, t].astype(F32), xin[1, t].astype(F32)], axis=1)

    for t in range(2, rows + 2):
        fill(slab1, t, row_in(t))

    @pl.when(me > 0)
    def _():
        up(0).wait_send()
        up(1).wait_send()
        down(0).wait_recv()
        down(1).wait_recv()

    @pl.when(me < np_ - 1)
    def _():
        down(0).wait_send()
        down(1).wait_send()
        up(0).wait_recv()
        up(1).wait_recv()

    for t in (0, 1, rows + 2, rows + 3):
        fill(slab1, t, row_in(t))

    w1 = w1_ref[...]
    w2 = w2_ref[core]
    depth = 9 * chans
    for t in range(rows + 2):
        first = mm(w1, slab1[t * 3 * chans : t * 3 * chans + depth, :])
        first = jnp.maximum(first, 0.0)
        if t == 0:
            first = jnp.where(me > 0, first, 0.0)
        if t == rows + 1:
            first = jnp.where(me < np_ - 1, first, 0.0)
        fill(slab2, t, first)

    dup = 128 // ch
    for t in range(rows):
        second = mm(w2, slab2[t * 3 * chans : t * 3 * chans + depth, :])
        second = jnp.maximum(second, 0.0).astype(BF16)
        for g in range(dup):
            hdup[t * 128 + g * ch : t * 128 + (g + 1) * ch, :] = second

    fwd = fwd_ref[...]
    group = lax.broadcasted_iota(jnp.int32, (np_, 128), 1) // ch
    for j in range(rows):
        s = mm(fwd, hdup[j * 128 : (j + 1) * 128, :], ((1,), (1,)))
        for xh in range(lane_w // 128):
            acc = s[xh * dup * np_ : (xh * dup + 1) * np_, :]
            for g in range(1, dup):
                at = (xh * dup + g) * np_
                acc = jnp.where(group == g, s[at : at + np_, :], acc)
            tb[xh, pl.ds(j, np_, stride=rows), :] = acc
    quad = quad_ref[me]
    for p in range(np_):
        piece = jnp.concatenate(
            [tb[xh, p * rows : (p + 1) * rows, :] for xh in range(lane_w // 128)], axis=1
        )
        send_b[p] = (piece * quad).astype(BF16)

    def b_copy(to_lat, to_core, from_lat, from_core):
        return pltpu.make_async_remote_copy(
            src_ref=send_b.at[to_lat], dst_ref=recv_b.at[from_core, from_lat],
            send_sem=b_send.at[to_core, to_lat], recv_sem=b_recv.at[from_core, from_lat],
            device_id={"lat": to_lat, "lon": to_core}, device_id_type=MESH,
        )

    def b_start(d, _):
        p = lax.rem(me + d, np_)
        for h in range(2):
            b_copy(p, (core + h) % 2, me, core).start()
        return 0

    lax.fori_loop(1, np_, b_start, 0)
    b_copy(me, other, me, core).start()
    recv_b[core, me] = send_b[me]

    def b_wait(d, _):
        q = lax.rem(me + np_ - d, np_)
        for h in range(2):
            b_copy(q, (core + h) % 2, q, (core + h) % 2).wait_recv()
        return 0

    b_copy(me, other, me, other).wait_recv()
    lax.fori_loop(1, np_, b_wait, 0)

    lt_b = lt[...].astype(BF16)
    x_lane = lax.broadcasted_iota(jnp.int32, (degrees, lane_w), 1) // ch
    halves = []
    for h in range(2):
        r = recv_b[h].astype(F32).reshape(lat_total, lane_w).astype(BF16)
        halves.append(mm(lt_b, r))
    for x in range(per_x):
        q = x // 2
        part = [jnp.where(x_lane == x, u[q * degrees : (q + 1) * degrees, :], 0.0).astype(BF16) for u in halves]
        spec[x * degrees : (x + 1) * degrees, :] = mm(jnp.concatenate(part, axis=1), sq_ref[...])

    sub = 8
    block = per_x * sub
    own = (
        lax.broadcasted_iota(jnp.int32, (block, sub * ch), 0) % sub
        == lax.broadcasted_iota(jnp.int32, (block, sub * ch), 1) // ch
    )
    for s in range(degrees // sub):
        lhs = jnp.concatenate(
            [spec[x * degrees + s * sub : x * degrees + (s + 1) * sub, :] for x in range(per_x)], axis=0
        ).astype(BF16)
        rhs = mix_ref[s * sub * ch : (s + 1) * sub * ch, :]
        both = jnp.where(own, mm(lhs, rhs, ((1,), (1,))), 0.0).astype(BF16)
        wide = mm(both, sp_ref[...])
        for x in range(per_x):
            mixed[x * degrees + s * sub : x * degrees + (s + 1) * sub, :] = wide[x * sub : (x + 1) * sub, :]

    own_row = (
        lax.broadcasted_iota(jnp.int32, (lat_total, lane_w), 0) % rows
        == lax.broadcasted_iota(jnp.int32, (lat_total, lane_w), 1) // ch
    )
    for x in range(per_x):
        y = mm(lg[x // 2], mixed[x * degrees : (x + 1) * degrees, :].astype(BF16))
        y = jnp.where(own_row, y, 0.0).astype(BF16)
        z = mm(pick_ref[...], y)
        for xh in range(lane_w // 128):
            tc[xh, pl.ds(x, np_, stride=per_x), :] = z[:, xh * 128 : (xh + 1) * 128]
    for p in range(np_):
        send_c[p] = jnp.concatenate(
            [tc[xh, p * per_x : (p + 1) * per_x, :] for xh in range(lane_w // 128)], axis=1
        ).astype(BF16)

    def c_copy(to_lat, from_lat):
        return pltpu.make_async_remote_copy(
            src_ref=send_c.at[to_lat], dst_ref=recv_c.at[from_lat],
            send_sem=c_send.at[to_lat], recv_sem=c_recv.at[from_lat],
            device_id={"lat": to_lat, "lon": core}, device_id_type=MESH,
        )

    def c_start(d, _):
        c_copy(lax.rem(me + d, np_), me).start()
        return 0

    lax.fori_loop(1, np_, c_start, 0)
    recv_c[me] = send_c[me]

    def b_done(d, _):
        p = lax.rem(me + d, np_)
        for h in range(2):
            b_copy(p, (core + h) % 2, me, core).wait_send()
        return 0

    b_copy(me, other, me, core).wait_send()
    lax.fori_loop(1, np_, b_done, 0)

    def c_wait(d, _):
        q = lax.rem(me + np_ - d, np_)
        c_copy(q, q).wait_recv()
        return 0

    lax.fori_loop(1, np_, c_wait, 0)
    full = recv_c[...].astype(F32).reshape(np_ * per_x, lane_w).T.astype(BF16)
    done = mm(full, inv_ref[...])
    for j in range(rows):
        out_ref[j] = done[j * ch : (j + 1) * ch, :].astype(BF16)

    def c_done(d, _):
        c_copy(lax.rem(me + d, np_), me).wait_send()
        return 0

    lax.fori_loop(1, np_, c_done, 0)


def local(np_, fields, conv_first, conv_second, mixing):
    chans, rows, half_w = fields.shape
    ch = chans // 2
    width = 2 * half_w
    lat_total = np_ * rows
    orders = lat_total // 2
    degrees = mixing.shape[0]
    per_x = 2 * orders // np_
    lane_w = per_x * ch
    tables = constant_tables(np_, rows, width, orders, lane_w, ch)
    x = jnp.transpose(fields, (1, 0, 2))
    w1 = jnp.transpose(conv_first, (0, 2, 3, 1)).reshape(chans, 9 * chans)
    w2 = jnp.transpose(conv_second, (0, 2, 3, 1)).reshape(2, ch, 9 * chans)
    mix = mixing.reshape(degrees * ch, chans)
    vm = pl.BlockSpec(memory_space=pltpu.VMEM)
    dma = pltpu.SemaphoreType.DMA
    out = pl.pallas_call(
        functools.partial(body, (np_, rows, chans, half_w, degrees)),
        out_shape=jax.ShapeDtypeStruct((rows, ch, width), BF16),
        in_specs=[vm] * 12,
        out_specs=vm,
        scratch_shapes=[
            pltpu.VMEM((2, rows + 4, chans, half_w), BF16),
            pltpu.VMEM(((rows + 4) * 3 * chans, width), BF16),
            pltpu.VMEM(((rows + 2) * 3 * chans, width), BF16),
            pltpu.VMEM((rows * 128, width), BF16),
            pltpu.VMEM((lane_w // 128, lat_total, 128), F32),
            pltpu.VMEM((np_, rows, lane_w), BF16),
            pltpu.VMEM((2, np_, rows, lane_w), BF16),
            pltpu.VMEM((per_x // 2 * degrees, lat_total), F32),
            pltpu.VMEM((per_x // 2, lat_total, degrees), BF16),
            pltpu.VMEM((per_x * degrees, chans), F32),
            pltpu.VMEM((lane_w // 128, np_ * per_x, 128), F32),
            pltpu.VMEM((np_, per_x, lane_w), BF16),
            pltpu.VMEM((np_, per_x, lane_w), BF16),
            pltpu.VMEM((per_x * degrees, lane_w), F32),
            dma((5,)), dma((5,)), dma((2, np_)), dma((2, np_)), dma((np_,)), dma((np_,)),
        ],
        compiler_params=pltpu.CompilerParams(
            collective_id=0, has_side_effects=True, vmem_limit_bytes=48 << 20
        ),
    )(x, w1, w2, mix, *tables)
    return jnp.transpose(out, (1, 0, 2))


def solution(mesh):
    in_specs = (P("groups", "lat", "lon"), P(), P(), P(None, "lon", None))
    out_specs = P(("groups", "lon"), "lat", None)
    return jax.shard_map(
        functools.partial(local, mesh.shape["lat"]),
        mesh=mesh, in_specs=in_specs, out_specs=out_specs, check_vma=False,
    )
```

```python
import functools
import math

import jax
import jax.numpy as jnp
import numpy as np
from jax import lax
from jax.experimental import pallas as pl
from jax.experimental.pallas import tpu as pltpu
from jax.sharding import PartitionSpec as P

MESH = pl.DeviceIdType.MESH
BF16 = jnp.bfloat16
F32 = jnp.float32


def mm(a, b, dims=((1,), (0,))):
    return lax.dot_general(a, b, (dims, ((), ())), preferred_element_type=F32)


def constant_tables(lat_count, rows, lon_total, orders, width):
    lat_total = lat_count * rows
    per_x = 2 * orders // lat_count
    k = np.arange(lon_total)[:, None]
    m = np.arange(orders)[None, :]
    angle = (k * m % lon_total).astype(np.float64) * (2.0 * math.pi / lon_total)
    forward = np.stack([np.cos(angle), -np.sin(angle)], axis=-1).reshape(lon_total, 2 * orders)
    factor = np.where(np.arange(orders) == 0, 1.0, 2.0)[:, None, None]
    inverse = np.stack([np.cos(angle.T), -np.sin(angle.T)], axis=1) * factor
    inverse = inverse.reshape(2 * orders, lon_total)
    forward = forward.T.reshape(lat_count, per_x, lon_total).transpose(1, 0, 2)
    forward = forward.reshape(2 * orders, lon_total)
    theta = (np.arange(lat_total) + 0.5) * (math.pi / lat_total)
    quad = np.sin(theta) * (math.pi / lat_total / lon_total)
    quad = np.broadcast_to(quad.reshape(lat_count, rows, 1), (lat_count, rows, width))
    half = lat_total // 2
    fold = np.concatenate([np.arange(half), np.arange(half)[::-1]])
    cosine = np.cos(theta[fold])[None, :]
    counter = np.arange(1, orders + 1)
    sums = np.concatenate([[0.0], np.cumsum(np.log((2.0 * counter - 1.0) / (2.0 * counter)))])
    ids = np.arange(orders)
    start = (0.5 * np.log(ids + 0.5) + 0.5 * sums[ids])[:, None] + ids[:, None] * np.log(np.sin(theta[fold]))[None, :]
    start = start.reshape(lat_count, per_x // 2, lat_total)
    start = np.pad(start, ((0, 0), (0, 8 - per_x // 2), (0, 0)))
    as_bf = lambda a: jnp.asarray(np.asarray(a, np.float32).astype(jnp.bfloat16))
    as_f = lambda a: jnp.asarray(np.ascontiguousarray(a, np.float32))
    return as_bf(forward), as_bf(inverse), as_f(quad), as_f(cosine), as_f(start)


def peers(np_, me):
    if np_ & (np_ - 1):
        return [lax.rem(me + d, np_) for d in range(np_ - 1, 0, -1)]
    out = []
    for d in range(np_ - 1, 0, -1):
        p, bit = me, 1
        while bit < np_:
            if d & bit:
                p = p + bit - 2 * bit * (me // bit % 2)
            bit *= 2
        out.append(p)
    return out


def body(sizes, x_ref, w1_ref, w2_ref, cos_ref, mix_hbm, fwd_hbm, inv_hbm, quad_hbm, start_hbm, out_ref,
         xin, slab1, slab2, hdup, tb, send_b, recv_b, lt, lt_b, lg, spec, tc, send_c, recv_c, mixed,
         w1s, w2s, sq_s, sp_s, mix_s, fwd_s, inv_s, quad_s, start_s,
         a_send, a_recv, b_send, b_recv, c_send, c_recv, l_sem):
    np_, rows, chans, half_w, degrees = sizes
    ch = chans // 2
    width = 2 * half_w
    per_x = 8
    orders_here = per_x // 2
    lat_total = np_ * rows
    lane_w = per_x * ch
    me = lax.axis_index("lat")
    core = lax.axis_index("lon")
    other = 1 - core

    barrier = pltpu.get_barrier_semaphore()

    others = peers(np_, me)
    pl.semaphore_signal(barrier, inc=1, device_id={"lat": me, "lon": other}, device_id_type=MESH)
    for p in others:
        for h in (core, other):
            pl.semaphore_signal(barrier, inc=1, device_id={"lat": p, "lon": h}, device_id_type=MESH)

    loads = [
        pltpu.make_async_copy(a, b, l_sem.at[k])
        for k, (a, b) in enumerate([
            (start_hbm.at[me], start_s), (quad_hbm.at[me], quad_s), (fwd_hbm, fwd_s),
            (mix_hbm, mix_s), (inv_hbm, inv_s),
        ])
    ]
    for load in loads:
        load.start()

    for k in range(9):
        at = slice(k * chans, (k + 1) * chans)
        w1s[:, at] = w1_ref[k // 3, k % 3]
        w2s[:, at] = w2_ref[k // 3, k % 3, pl.ds(pl.multiple_of(core * ch, ch), ch), :]

    pl.semaphore_wait(barrier, 2 * np_ - 1)

    def across():
        return pltpu.make_async_remote_copy(
            src_ref=x_ref, dst_ref=xin.at[core, pl.ds(2, rows)],
            send_sem=a_send.at[4], recv_sem=a_recv.at[4],
            device_id={"lat": me, "lon": other}, device_id_type=MESH,
        )

    def up(h):
        return pltpu.make_async_remote_copy(
            src_ref=x_ref.at[pl.ds(0, 2)], dst_ref=xin.at[core, pl.ds(rows + 2, 2)],
            send_sem=a_send.at[h], recv_sem=a_recv.at[h],
            device_id={"lat": jnp.maximum(me - 1, 0), "lon": (core + h) % 2}, device_id_type=MESH,
        )

    def down(h):
        return pltpu.make_async_remote_copy(
            src_ref=x_ref.at[pl.ds(rows - 2, 2)], dst_ref=xin.at[core, pl.ds(0, 2)],
            send_sem=a_send.at[2 + h], recv_sem=a_recv.at[2 + h],
            device_id={"lat": jnp.minimum(me + 1, np_ - 1), "lon": (core + h) % 2}, device_id_type=MESH,
        )

    @pl.when(me > 0)
    def _():
        up(0).start()
        up(1).start()

    @pl.when(me < np_ - 1)
    def _():
        down(0).start()
        down(1).start()

    across().start()

    @pl.when(me == 0)
    def _():
        xin[:, pl.ds(0, 2)] = jnp.zeros((2, 2, chans, half_w), BF16)

    @pl.when(me == np_ - 1)
    def _():
        xin[:, pl.ds(rows + 2, 2)] = jnp.zeros((2, 2, chans, half_w), BF16)

    xin[core, pl.ds(2, rows)] = x_ref[...]

    loads[0].wait()
    cosine = cos_ref[...]
    log_start = start_s[...]
    wide_l = (8, degrees)
    order = (lax.broadcasted_iota(jnp.int32, wide_l, 0) + me * orders_here).astype(F32)
    degree = lax.broadcasted_iota(jnp.int32, wide_l, 1).astype(F32)
    earlier = degree - 1.0
    coef_a = jnp.sqrt(
        jnp.maximum(4.0 * degree * degree - 1.0, 1.0) / jnp.maximum(degree * degree - order * order, 1.0)
    )
    coef_b = coef_a * jnp.sqrt(
        jnp.maximum(earlier * earlier - order * order, 0.0) / jnp.maximum(4.0 * earlier * earlier - 1.0, 1.0)
    )
    wide_j = (8, lat_total)
    order_id = lax.broadcasted_iota(jnp.int32, wide_j, 0) + me * orders_here
    southern = lax.broadcasted_iota(jnp.int32, wide_j, 1) >= lat_total // 2
    sign_even = jnp.where(southern & (order_id % 2 == 1), -1.0, 1.0)
    sign_odd = jnp.where(southern & (order_id % 2 == 0), -1.0, 1.0)
    start_scale = jnp.exp(log_start)
    span = 32 if degrees % 32 == 0 else degrees
    current = previous = log_scale = scale = jnp.zeros(wide_j, F32)
    for l_id in range(degrees):
        is_start = order_id == l_id
        newest = (
            (coef_a[:, l_id : l_id + 1] * cosine) * current
            - coef_b[:, l_id : l_id + 1] * previous
            + jnp.where(is_start, 1.0, 0.0)
        )
        scale = jnp.where(is_start, start_scale, scale)
        previous, current = current, newest
        value = newest * (scale * (sign_odd if l_id % 2 else sign_even))
        for v in range(lat_total // 128):
            lt[v, l_id * 8 : (l_id + 1) * 8, :] = value[:, v * 128 : (v + 1) * 128]
        if (l_id + 1) % span == 0 and l_id + 1 < degrees:
            log_scale = jnp.where((order_id > l_id - span) & (order_id <= l_id), log_start, log_scale)
            size_now = jnp.maximum(jnp.abs(current), jnp.abs(previous))
            safe = jnp.where(size_now > 0.0, size_now, 1.0)
            current = current / safe
            previous = previous / safe
            log_scale = log_scale + jnp.log(safe)
            scale = jnp.exp(log_scale)
    across().wait()

    def fill(slab, t, wide):
        base = t * 3 * chans
        slab[base : base + chans, :] = pltpu.roll(wide, 1, 1).astype(BF16)
        slab[base + chans : base + 2 * chans, :] = wide.astype(BF16)
        slab[base + 2 * chans : base + 3 * chans, :] = pltpu.roll(wide, width - 1, 1).astype(BF16)

    def row_in(t):
        return jnp.concatenate([xin[0, t].astype(F32), xin[1, t].astype(F32)], axis=1)

    for t in range(2, rows + 2):
        fill(slab1, t, row_in(t))

    @pl.when(me > 0)
    def _():
        up(0).wait_send()
        up(1).wait_send()
        down(0).wait_recv()
        down(1).wait_recv()

    @pl.when(me < np_ - 1)
    def _():
        down(0).wait_send()
        down(1).wait_send()
        up(0).wait_recv()
        up(1).wait_recv()

    for t in (0, 1, rows + 2, rows + 3):
        fill(slab1, t, row_in(t))

    w1 = w1s[...]
    w2 = w2s[...]
    depth = 9 * chans
    for t in range(rows + 2):
        first = mm(w1, slab1[t * 3 * chans : t * 3 * chans + depth, :])
        first = jnp.maximum(first, 0.0)
        if t == 0:
            first = jnp.where(me > 0, first, 0.0)
        if t == rows + 1:
            first = jnp.where(me < np_ - 1, first, 0.0)
        fill(slab2, t, first)

    dup = 128 // ch
    for t in range(rows):
        second = mm(w2, slab2[t * 3 * chans : t * 3 * chans + depth, :])
        second = jnp.maximum(second, 0.0).astype(BF16)
        for g in range(dup):
            hdup[t * 128 + g * ch : t * 128 + (g + 1) * ch, :] = second

    loads[1].wait()
    loads[2].wait()
    fwd = fwd_s[...]
    group = lax.broadcasted_iota(jnp.int32, (np_, 128), 1) // ch
    for j in range(rows):
        s = mm(fwd, hdup[j * 128 : (j + 1) * 128, :], ((1,), (1,)))
        for xh in range(lane_w // 128):
            acc = s[xh * dup * np_ : (xh * dup + 1) * np_, :]
            for g in range(1, dup):
                at = (xh * dup + g) * np_
                acc = jnp.where(group == g, s[at : at + np_, :], acc)
            tb[xh, pl.ds(j, np_, stride=rows), :] = acc
    quad = quad_s[...]
    for p in range(np_):
        piece = jnp.concatenate(
            [tb[xh, p * rows : (p + 1) * rows, :] for xh in range(lane_w // 128)], axis=1
        )
        send_b[p] = (piece * quad).astype(BF16)

    def b_copy(to_lat, to_core, from_lat, from_core):
        return pltpu.make_async_remote_copy(
            src_ref=send_b.at[to_lat], dst_ref=recv_b.at[from_core, from_lat],
            send_sem=b_send.at[to_core, to_lat], recv_sem=b_recv.at[from_core, from_lat],
            device_id={"lat": to_lat, "lon": to_core}, device_id_type=MESH,
        )

    for p in others:
        for h in (core, other):
            b_copy(p, h, me, core).start()
    b_copy(me, other, me, core).start()
    recv_b[core, me] = send_b[me]

    for q in range(orders_here):
        table = jnp.concatenate(
            [lt[v, pl.ds(q, degrees, stride=8), :] for v in range(lat_total // 128)], axis=1
        )
        lt_b[q * degrees : (q + 1) * degrees, :] = table.astype(BF16)
        lg[q] = table.T.astype(BF16)
    at = lax.broadcasted_iota(jnp.int32, (2 * lane_w, chans), 0)
    place = at // lane_w * ch + at % ch
    sq_s[...] = jnp.where(
        place == lax.broadcasted_iota(jnp.int32, (2 * lane_w, chans), 1), 1.0, 0.0
    ).astype(BF16)
    sp_s[...] = jnp.where(
        lax.broadcasted_iota(jnp.int32, (lane_w, rows * ch), 0) % ch
        == lax.broadcasted_iota(jnp.int32, (lane_w, rows * ch), 1) // rows, 1.0, 0.0
    ).astype(BF16)
    pick = jnp.where(
        lax.broadcasted_iota(jnp.int32, (np_, lat_total), 0)
        == lax.broadcasted_iota(jnp.int32, (np_, lat_total), 1) // rows, 1.0, 0.0
    ).astype(BF16)
    loads[3].wait()
    loads[4].wait()

    b_copy(me, other, me, other).wait_recv()
    for q in reversed(others):
        for h in (core, other):
            b_copy(q, h, q, h).wait_recv()

    table = lt_b[...]
    x_lane = lax.broadcasted_iota(jnp.int32, (degrees, lane_w), 1) // ch
    halves = []
    for h in range(2):
        r = recv_b[h].astype(F32).reshape(lat_total, lane_w).astype(BF16)
        halves.append(mm(table, r))
    for x in range(per_x):
        q = x // 2
        part = [jnp.where(x_lane == x, u[q * degrees : (q + 1) * degrees, :], 0.0).astype(BF16) for u in halves]
        spec[x * degrees : (x + 1) * degrees, :] = mm(jnp.concatenate(part, axis=1), sq_s[...])

    sub = 8
    block = per_x * sub
    own = (
        lax.broadcasted_iota(jnp.int32, (block, sub * ch), 0) % sub
        == lax.broadcasted_iota(jnp.int32, (block, sub * ch), 1) // ch
    )
    for s in range(degrees // sub):
        lhs = jnp.concatenate(
            [spec[x * degrees + s * sub : x * degrees + (s + 1) * sub, :] for x in range(per_x)], axis=0
        ).astype(BF16)
        rhs = mix_s[s * sub * ch : (s + 1) * sub * ch, :]
        both = jnp.where(own, mm(lhs, rhs, ((1,), (1,))), 0.0).astype(BF16)
        wide = mm(both, sp_s[...])
        for x in range(per_x):
            mixed[x * degrees + s * sub : x * degrees + (s + 1) * sub, :] = wide[x * sub : (x + 1) * sub, :]

    own_row = (
        lax.broadcasted_iota(jnp.int32, (lat_total, lane_w), 0) % rows
        == lax.broadcasted_iota(jnp.int32, (lat_total, lane_w), 1) % rows
    )
    for x in range(per_x):
        y = mm(lg[x // 2], mixed[x * degrees : (x + 1) * degrees, :].astype(BF16))
        y = jnp.where(own_row, y, 0.0).astype(BF16)
        z = mm(pick, y)
        for xh in range(lane_w // 128):
            tc[xh, pl.ds(x, np_, stride=per_x), :] = z[:, xh * 128 : (xh + 1) * 128]
    for p in range(np_):
        send_c[p] = jnp.concatenate(
            [tc[xh, p * per_x : (p + 1) * per_x, :] for xh in range(lane_w // 128)], axis=1
        ).astype(BF16)

    def c_copy(to_lat, from_lat):
        return pltpu.make_async_remote_copy(
            src_ref=send_c.at[to_lat], dst_ref=recv_c.at[from_lat],
            send_sem=c_send.at[to_lat], recv_sem=c_recv.at[from_lat],
            device_id={"lat": to_lat, "lon": core}, device_id_type=MESH,
        )

    for p in others:
        c_copy(p, me).start()
    recv_c[me] = send_c[me]

    b_copy(me, other, me, core).wait_send()
    for p in others:
        for h in (core, other):
            b_copy(p, h, me, core).wait_send()

    for q in reversed(others):
        c_copy(q, q).wait_recv()
    full = recv_c[...].astype(F32).reshape(np_ * per_x, lane_w).T.astype(BF16)
    out_ref[...] = mm(full, inv_s[...]).astype(BF16)
    for p in others:
        c_copy(p, me).wait_send()


def local(np_, fields, conv_first, conv_second, mixing):
    chans, rows, half_w = fields.shape
    ch = chans // 2
    width = 2 * half_w
    lat_total = np_ * rows
    orders = lat_total // 2
    degrees = mixing.shape[0]
    per_x = 2 * orders // np_
    lane_w = per_x * ch
    forward, inverse, quad, cosine, start = constant_tables(np_, rows, width, orders, lane_w)
    x = jnp.transpose(fields, (1, 0, 2))
    w1 = jnp.transpose(conv_first, (2, 3, 0, 1))
    w2 = jnp.transpose(conv_second, (2, 3, 0, 1))
    mix = mixing.reshape(degrees * ch, chans)
    vm = pl.BlockSpec(memory_space=pltpu.VMEM)
    hbm = pl.BlockSpec(memory_space=pltpu.HBM)
    dma = pltpu.SemaphoreType.DMA
    out = pl.pallas_call(
        functools.partial(body, (np_, rows, chans, half_w, degrees)),
        out_shape=jax.ShapeDtypeStruct((ch * rows, width), BF16),
        in_specs=[vm] * 4 + [hbm] * 5,
        out_specs=vm,
        scratch_shapes=[
            pltpu.VMEM((2, rows + 4, chans, half_w), BF16),
            pltpu.VMEM(((rows + 4) * 3 * chans, width), BF16),
            pltpu.VMEM(((rows + 2) * 3 * chans, width), BF16),
            pltpu.VMEM((rows * 128, width), BF16),
            pltpu.VMEM((lane_w // 128, lat_total, 128), F32),
            pltpu.VMEM((np_, rows, lane_w), BF16),
            pltpu.VMEM((2, np_, rows, lane_w), BF16),
            pltpu.VMEM((lat_total // 128, 8 * degrees, 128), F32),
            pltpu.VMEM((per_x // 2 * degrees, lat_total), BF16),
            pltpu.VMEM((per_x // 2, lat_total, degrees), BF16),
            pltpu.VMEM((per_x * degrees, chans), F32),
            pltpu.VMEM((lane_w // 128, np_ * per_x, 128), F32),
            pltpu.VMEM((np_, per_x, lane_w), BF16),
            pltpu.VMEM((np_, per_x, lane_w), BF16),
            pltpu.VMEM((per_x * degrees, lane_w), F32),
            pltpu.VMEM((chans, 9 * chans), BF16),
            pltpu.VMEM((ch, 9 * chans), BF16),
            pltpu.VMEM((2 * lane_w, chans), BF16),
            pltpu.VMEM((lane_w, lane_w), BF16),
            pltpu.VMEM((degrees * ch, chans), BF16),
            pltpu.VMEM((2 * orders, width), BF16),
            pltpu.VMEM((2 * orders, width), BF16),
            pltpu.VMEM((rows, lane_w), F32),
            pltpu.VMEM((8, lat_total), F32),
            dma((5,)), dma((5,)), dma((2, np_)), dma((2, np_)), dma((np_,)), dma((np_,)), dma((5,)),
        ],
        compiler_params=pltpu.CompilerParams(
            collective_id=0, has_side_effects=True, vmem_limit_bytes=48 << 20
        ),
    )(x, w1, w2, cosine, mix, forward, inverse, quad, start)
    return out.reshape(ch, rows, width)


def solution(mesh):
    in_specs = (P("groups", "lat", "lon"), P(), P(), P(None, "lon", None))
    out_specs = P(("groups", "lon"), "lat", None)
    return jax.shard_map(
        functools.partial(local, mesh.shape["lat"]),
        mesh=mesh, in_specs=in_specs, out_specs=out_specs, check_vma=False,
    )
```

```python
import functools
import math

import jax
import jax.numpy as jnp
import numpy as np
from jax import lax
from jax.experimental import pallas as pl
from jax.experimental.pallas import tpu as pltpu
from jax.sharding import PartitionSpec as P

MESH = pl.DeviceIdType.MESH
BF16 = jnp.bfloat16
F32 = jnp.float32


def mm(a, b, dims=((1,), (0,))):
    return lax.dot_general(a, b, (dims, ((), ())), preferred_element_type=F32)


def constant_tables(lat_count, rows, lon_total, orders, width):
    lat_total = lat_count * rows
    per_x = 2 * orders // lat_count
    k = np.arange(lon_total)[:, None]
    m = np.arange(orders)[None, :]
    angle = (k * m % lon_total).astype(np.float64) * (2.0 * math.pi / lon_total)
    forward = np.stack([np.cos(angle), -np.sin(angle)], axis=-1).reshape(lon_total, 2 * orders)
    factor = np.where(np.arange(orders) == 0, 1.0, 2.0)[:, None, None]
    inverse = np.stack([np.cos(angle.T), -np.sin(angle.T)], axis=1) * factor
    inverse = inverse.reshape(2 * orders, lon_total)
    forward = forward.T.reshape(lat_count, per_x, lon_total).transpose(1, 0, 2)
    forward = forward.reshape(2 * orders, lon_total)
    theta = (np.arange(lat_total) + 0.5) * (math.pi / lat_total)
    quad = np.sin(theta) * (math.pi / lat_total / lon_total)
    quad = np.broadcast_to(quad.reshape(lat_count, rows, 1), (lat_count, rows, width))
    half = lat_total // 2
    fold = np.concatenate([np.arange(half), np.arange(half)[::-1]])
    cosine = np.cos(theta[fold])[None, :]
    counter = np.arange(1, orders + 1)
    sums = np.concatenate([[0.0], np.cumsum(np.log((2.0 * counter - 1.0) / (2.0 * counter)))])
    ids = np.arange(orders)
    start = (0.5 * np.log(ids + 0.5) + 0.5 * sums[ids])[:, None] + ids[:, None] * np.log(np.sin(theta[fold]))[None, :]
    start = start.reshape(lat_count, per_x // 2, lat_total)
    start = np.pad(start, ((0, 0), (0, 8 - per_x // 2), (0, 0)))
    start[:, 7] = cosine
    as_bf = lambda a: jnp.asarray(np.asarray(a, np.float32).astype(jnp.bfloat16))
    as_f = lambda a: jnp.asarray(np.ascontiguousarray(a, np.float32))
    return as_bf(forward), as_bf(inverse), as_f(quad), as_f(start)


def peers(np_, me):
    if np_ & (np_ - 1):
        return [lax.rem(me + d, np_) for d in range(np_ - 1, 0, -1)]
    out = []
    for d in range(np_ - 1, 0, -1):
        p, bit = me, 1
        while bit < np_:
            if d & bit:
                p = p + bit - 2 * bit * (me // bit % 2)
            bit *= 2
        out.append(p)
    return out


def body(sizes, x_hbm, w1_hbm, w2_hbm, mix_hbm, fwd_hbm, inv_hbm, quad_hbm, start_hbm, out_ref,
         xin, slab1, slab2, hdup, tb, send_b, recv_b, lt, lt_b, lg, spec, tc, send_c, recv_c, mixed,
         x_s, x32, x_ref, w1_ref, w2_ref, w1s, w2s, sq_s, sp_s, mix_s, fwd_s, inv_s, quad_s, start_s,
         a_send, a_recv, b_send, b_recv, c_send, c_recv, l_sem, ready):
    np_, rows, chans, half_w, degrees = sizes
    ch = chans // 2
    width = 2 * half_w
    per_x = 8
    orders_here = per_x // 2
    lat_total = np_ * rows
    lane_w = per_x * ch
    me = lax.axis_index("lat")
    core = lax.axis_index("lon")
    other = 1 - core

    barrier = pltpu.get_barrier_semaphore()

    others = peers(np_, me)

    def greet(p, h):
        pl.semaphore_signal(barrier, inc=1, device_id={"lat": p, "lon": h}, device_id_type=MESH)

    near = 1
    while near * near < np_ or np_ % near:
        near += 1
    far = np_ // near
    place = me % near
    far_others = [(me + near * d) % np_ for d in range(1, far)]
    crosses_up = (place == 0) & (me > 0)
    crosses_down = (place == near - 1) & (me < np_ - 1)
    for p in far_others:
        greet(p, core)

    @pl.when(crosses_up)
    def _():
        greet(me - 1, core)
        greet(me - 1, other)

    @pl.when(crosses_down)
    def _():
        greet(me + 1, core)
        greet(me + 1, other)

    for d in range(1, near):
        p = me - place + (place + d) % near
        greet(p, core)
        greet(p, other)
    greet(me, other)

    loads = [
        pltpu.make_async_copy(a, b, l_sem.at[k])
        for k, (a, b) in enumerate([
            (start_hbm.at[me], start_s), (quad_hbm.at[me], quad_s), (fwd_hbm, fwd_s),
            (mix_hbm, mix_s), (inv_hbm, inv_s), (x_hbm, x_s), (w1_hbm, w1_ref), (w2_hbm, w2_ref),
        ])
    ]
    for k in (5, 6, 7, 0, 1, 2, 3, 4):
        loads[k].start()

    for k in (5, 6, 7):
        loads[k].wait()
    for v in range(half_w // 128):
        x32[v] = x_s[:, :, v * 128 : (v + 1) * 128].astype(F32).reshape(chans * rows, 128)
        for t in range(rows):
            x_ref[t, :, v * 128 : (v + 1) * 128] = x32[v, pl.ds(t, chans, stride=rows), :].astype(BF16)
    for k in range(9):
        at = slice(k * chans, (k + 1) * chans)
        w1s[:, at] = w1_ref[k // 3, k % 3]
        w2s[:, at] = w2_ref[k // 3, k % 3, pl.ds(pl.multiple_of(core * ch, ch), ch), :]

    known = 2 * near - 1 + far - 1
    pl.semaphore_wait(
        barrier, known + 2 * crosses_up.astype(jnp.int32) + 2 * crosses_down.astype(jnp.int32)
    )

    def across():
        return pltpu.make_async_remote_copy(
            src_ref=x_ref, dst_ref=xin.at[core, pl.ds(2, rows)],
            send_sem=a_send.at[4], recv_sem=a_recv.at[4],
            device_id={"lat": me, "lon": other}, device_id_type=MESH,
        )

    def up(h):
        return pltpu.make_async_remote_copy(
            src_ref=x_ref.at[pl.ds(0, 2)], dst_ref=xin.at[core, pl.ds(rows + 2, 2)],
            send_sem=a_send.at[h], recv_sem=a_recv.at[h],
            device_id={"lat": jnp.maximum(me - 1, 0), "lon": (core + h) % 2}, device_id_type=MESH,
        )

    def down(h):
        return pltpu.make_async_remote_copy(
            src_ref=x_ref.at[pl.ds(rows - 2, 2)], dst_ref=xin.at[core, pl.ds(0, 2)],
            send_sem=a_send.at[2 + h], recv_sem=a_recv.at[2 + h],
            device_id={"lat": jnp.minimum(me + 1, np_ - 1), "lon": (core + h) % 2}, device_id_type=MESH,
        )

    @pl.when(me > 0)
    def _():
        up(0).start()
        up(1).start()

    @pl.when(me < np_ - 1)
    def _():
        down(0).start()
        down(1).start()

    across().start()

    for p in far_others:
        pl.semaphore_signal(ready, inc=1, device_id={"lat": p, "lon": core}, device_id_type=MESH)

    @pl.when(me == 0)
    def _():
        xin[:, pl.ds(0, 2)] = jnp.zeros((2, 2, chans, half_w), BF16)

    @pl.when(me == np_ - 1)
    def _():
        xin[:, pl.ds(rows + 2, 2)] = jnp.zeros((2, 2, chans, half_w), BF16)

    xin[core, pl.ds(2, rows)] = x_ref[...]

    loads[0].wait()
    cosine = start_s[7:8, :]
    log_start = start_s[...]
    wide_l = (8, degrees)
    order = (lax.broadcasted_iota(jnp.int32, wide_l, 0) + me * orders_here).astype(F32)
    degree = lax.broadcasted_iota(jnp.int32, wide_l, 1).astype(F32)
    earlier = degree - 1.0
    coef_a = jnp.sqrt(
        jnp.maximum(4.0 * degree * degree - 1.0, 1.0) / jnp.maximum(degree * degree - order * order, 1.0)
    )
    coef_b = coef_a * jnp.sqrt(
        jnp.maximum(earlier * earlier - order * order, 0.0) / jnp.maximum(4.0 * earlier * earlier - 1.0, 1.0)
    )
    wide_j = (8, lat_total)
    order_id = lax.broadcasted_iota(jnp.int32, wide_j, 0) + me * orders_here
    southern = lax.broadcasted_iota(jnp.int32, wide_j, 1) >= lat_total // 2
    sign_even = jnp.where(southern & (order_id % 2 == 1), -1.0, 1.0)
    sign_odd = jnp.where(southern & (order_id % 2 == 0), -1.0, 1.0)
    start_scale = jnp.exp(log_start)
    span = 32 if degrees % 32 == 0 else degrees
    current = previous = log_scale = scale = jnp.zeros(wide_j, F32)
    for l_id in range(degrees):
        is_start = order_id == l_id
        newest = (
            (coef_a[:, l_id : l_id + 1] * cosine) * current
            - coef_b[:, l_id : l_id + 1] * previous
            + jnp.where(is_start, 1.0, 0.0)
        )
        scale = jnp.where(is_start, start_scale, scale)
        previous, current = current, newest
        value = newest * (scale * (sign_odd if l_id % 2 else sign_even))
        for v in range(lat_total // 128):
            lt[v, l_id * 8 : (l_id + 1) * 8, :] = value[:, v * 128 : (v + 1) * 128]
        if (l_id + 1) % span == 0 and l_id + 1 < degrees:
            log_scale = jnp.where((order_id > l_id - span) & (order_id <= l_id), log_start, log_scale)
            size_now = jnp.maximum(jnp.abs(current), jnp.abs(previous))
            safe = jnp.where(size_now > 0.0, size_now, 1.0)
            current = current / safe
            previous = previous / safe
            log_scale = log_scale + jnp.log(safe)
            scale = jnp.exp(log_scale)
    across().wait()

    def fill(slab, t, wide):
        base = t * 3 * chans
        slab[base : base + chans, :] = pltpu.roll(wide, 1, 1).astype(BF16)
        slab[base + chans : base + 2 * chans, :] = wide.astype(BF16)
        slab[base + 2 * chans : base + 3 * chans, :] = pltpu.roll(wide, width - 1, 1).astype(BF16)

    def row_in(t):
        return jnp.concatenate([xin[0, t].astype(F32), xin[1, t].astype(F32)], axis=1)

    for t in range(2, rows + 2):
        fill(slab1, t, row_in(t))

    @pl.when(me > 0)
    def _():
        up(0).wait_send()
        up(1).wait_send()
        down(0).wait_recv()
        down(1).wait_recv()

    @pl.when(me < np_ - 1)
    def _():
        down(0).wait_send()
        down(1).wait_send()
        up(0).wait_recv()
        up(1).wait_recv()

    for t in (0, 1, rows + 2, rows + 3):
        fill(slab1, t, row_in(t))

    w1 = w1s[...]
    w2 = w2s[...]
    depth = 9 * chans
    for t in range(rows + 2):
        first = mm(w1, slab1[t * 3 * chans : t * 3 * chans + depth, :])
        first = jnp.maximum(first, 0.0)
        if t == 0:
            first = jnp.where(me > 0, first, 0.0)
        if t == rows + 1:
            first = jnp.where(me < np_ - 1, first, 0.0)
        fill(slab2, t, first)

    dup = 128 // ch
    for t in range(rows):
        second = mm(w2, slab2[t * 3 * chans : t * 3 * chans + depth, :])
        second = jnp.maximum(second, 0.0).astype(BF16)
        for g in range(dup):
            hdup[t * 128 + g * ch : t * 128 + (g + 1) * ch, :] = second

    loads[1].wait()
    loads[2].wait()
    fwd = fwd_s[...]
    group = lax.broadcasted_iota(jnp.int32, (np_, 128), 1) // ch
    for j in range(rows):
        s = mm(fwd, hdup[j * 128 : (j + 1) * 128, :], ((1,), (1,)))
        for xh in range(lane_w // 128):
            acc = s[xh * dup * np_ : (xh * dup + 1) * np_, :]
            for g in range(1, dup):
                at = (xh * dup + g) * np_
                acc = jnp.where(group == g, s[at : at + np_, :], acc)
            tb[xh, pl.ds(j, np_, stride=rows), :] = acc
    quad = quad_s[...]
    for p in range(np_):
        piece = jnp.concatenate(
            [tb[xh, p * rows : (p + 1) * rows, :] for xh in range(lane_w // 128)], axis=1
        )
        send_b[p] = (piece * quad).astype(BF16)

    pl.semaphore_wait(ready, far - 1)

    def b_copy(to_lat, to_core, from_lat, from_core):
        return pltpu.make_async_remote_copy(
            src_ref=send_b.at[to_lat], dst_ref=recv_b.at[from_core, from_lat],
            send_sem=b_send.at[to_core, to_lat], recv_sem=b_recv.at[from_core, from_lat],
            device_id={"lat": to_lat, "lon": to_core}, device_id_type=MESH,
        )

    for p in others:
        for h in (core, other):
            b_copy(p, h, me, core).start()
    b_copy(me, other, me, core).start()
    recv_b[core, me] = send_b[me]

    for q in range(orders_here):
        table = jnp.concatenate(
            [lt[v, pl.ds(q, degrees, stride=8), :] for v in range(lat_total // 128)], axis=1
        )
        lt_b[q * degrees : (q + 1) * degrees, :] = table.astype(BF16)
        lg[q] = table.T.astype(BF16)
    at = lax.broadcasted_iota(jnp.int32, (2 * lane_w, chans), 0)
    place = at // lane_w * ch + at % ch
    sq_s[...] = jnp.where(
        place == lax.broadcasted_iota(jnp.int32, (2 * lane_w, chans), 1), 1.0, 0.0
    ).astype(BF16)
    sp_s[...] = jnp.where(
        lax.broadcasted_iota(jnp.int32, (lane_w, rows * ch), 0) % ch
        == lax.broadcasted_iota(jnp.int32, (lane_w, rows * ch), 1) // rows, 1.0, 0.0
    ).astype(BF16)
    pick = jnp.where(
        lax.broadcasted_iota(jnp.int32, (np_, lat_total), 0)
        == lax.broadcasted_iota(jnp.int32, (np_, lat_total), 1) // rows, 1.0, 0.0
    ).astype(BF16)
    loads[3].wait()
    loads[4].wait()

    b_copy(me, other, me, other).wait_recv()
    for q in reversed(others):
        for h in (core, other):
            b_copy(q, h, q, h).wait_recv()

    table = lt_b[...]
    x_lane = lax.broadcasted_iota(jnp.int32, (degrees, lane_w), 1) // ch
    halves = []
    for h in range(2):
        r = recv_b[h].astype(F32).reshape(lat_total, lane_w).astype(BF16)
        halves.append(mm(table, r))
    for x in range(per_x):
        q = x // 2
        part = [jnp.where(x_lane == x, u[q * degrees : (q + 1) * degrees, :], 0.0).astype(BF16) for u in halves]
        spec[x * degrees : (x + 1) * degrees, :] = mm(jnp.concatenate(part, axis=1), sq_s[...])

    sub = 8
    block = per_x * sub
    own = (
        lax.broadcasted_iota(jnp.int32, (block, sub * ch), 0) % sub
        == lax.broadcasted_iota(jnp.int32, (block, sub * ch), 1) // ch
    )
    for s in range(degrees // sub):
        lhs = jnp.concatenate(
            [spec[x * degrees + s * sub : x * degrees + (s + 1) * sub, :] for x in range(per_x)], axis=0
        ).astype(BF16)
        rhs = mix_s[s * sub * ch : (s + 1) * sub * ch, :]
        both = jnp.where(own, mm(lhs, rhs, ((1,), (1,))), 0.0).astype(BF16)
        wide = mm(both, sp_s[...])
        for x in range(per_x):
            mixed[x * degrees + s * sub : x * degrees + (s + 1) * sub, :] = wide[x * sub : (x + 1) * sub, :]

    own_row = (
        lax.broadcasted_iota(jnp.int32, (lat_total, lane_w), 0) % rows
        == lax.broadcasted_iota(jnp.int32, (lat_total, lane_w), 1) % rows
    )
    for x in range(per_x):
        y = mm(lg[x // 2], mixed[x * degrees : (x + 1) * degrees, :].astype(BF16))
        y = jnp.where(own_row, y, 0.0).astype(BF16)
        z = mm(pick, y)
        for xh in range(lane_w // 128):
            tc[xh, pl.ds(x, np_, stride=per_x), :] = z[:, xh * 128 : (xh + 1) * 128]
    for p in range(np_):
        send_c[p] = jnp.concatenate(
            [tc[xh, p * per_x : (p + 1) * per_x, :] for xh in range(lane_w // 128)], axis=1
        ).astype(BF16)

    def c_copy(to_lat, from_lat):
        return pltpu.make_async_remote_copy(
            src_ref=send_c.at[to_lat], dst_ref=recv_c.at[from_lat],
            send_sem=c_send.at[to_lat], recv_sem=c_recv.at[from_lat],
            device_id={"lat": to_lat, "lon": core}, device_id_type=MESH,
        )

    for p in others:
        c_copy(p, me).start()
    recv_c[me] = send_c[me]

    b_copy(me, other, me, core).wait_send()
    for p in others:
        for h in (core, other):
            b_copy(p, h, me, core).wait_send()

    for q in reversed(others):
        c_copy(q, q).wait_recv()
    full = recv_c[...].astype(F32).reshape(np_ * per_x, lane_w).T.astype(BF16)
    out_ref[...] = mm(full, inv_s[...]).astype(BF16)
    for p in others:
        c_copy(p, me).wait_send()


def local(np_, fields, conv_first, conv_second, mixing):
    chans, rows, half_w = fields.shape
    ch = chans // 2
    width = 2 * half_w
    lat_total = np_ * rows
    orders = lat_total // 2
    degrees = mixing.shape[0]
    per_x = 2 * orders // np_
    lane_w = per_x * ch
    forward, inverse, quad, start = constant_tables(np_, rows, width, orders, lane_w)
    w1 = jnp.transpose(conv_first, (2, 3, 0, 1))
    w2 = jnp.transpose(conv_second, (2, 3, 0, 1))
    mix = mixing.reshape(degrees * ch, chans)
    vm = pl.BlockSpec(memory_space=pltpu.VMEM)
    hbm = pl.BlockSpec(memory_space=pl.ANY)
    dma = pltpu.SemaphoreType.DMA
    out = pl.pallas_call(
        functools.partial(body, (np_, rows, chans, half_w, degrees)),
        out_shape=jax.ShapeDtypeStruct((ch * rows, width), BF16),
        in_specs=[hbm] * 8,
        out_specs=vm,
        scratch_shapes=[
            pltpu.VMEM((2, rows + 4, chans, half_w), BF16),
            pltpu.VMEM(((rows + 4) * 3 * chans, width), BF16),
            pltpu.VMEM(((rows + 2) * 3 * chans, width), BF16),
            pltpu.VMEM((rows * 128, width), BF16),
            pltpu.VMEM((lane_w // 128, lat_total, 128), F32),
            pltpu.VMEM((np_, rows, lane_w), BF16),
            pltpu.VMEM((2, np_, rows, lane_w), BF16),
            pltpu.VMEM((lat_total // 128, 8 * degrees, 128), F32),
            pltpu.VMEM((per_x // 2 * degrees, lat_total), BF16),
            pltpu.VMEM((per_x // 2, lat_total, degrees), BF16),
            pltpu.VMEM((per_x * degrees, chans), F32),
            pltpu.VMEM((lane_w // 128, np_ * per_x, 128), F32),
            pltpu.VMEM((np_, per_x, lane_w), BF16),
            pltpu.VMEM((np_, per_x, lane_w), BF16),
            pltpu.VMEM((per_x * degrees, lane_w), F32),
            pltpu.VMEM((chans, rows, half_w), BF16),
            pltpu.VMEM((half_w // 128, chans * rows, 128), F32),
            pltpu.VMEM((rows, chans, half_w), BF16),
            pltpu.VMEM((3, 3, chans, chans), BF16),
            pltpu.VMEM((3, 3, chans, chans), BF16),
            pltpu.VMEM((chans, 9 * chans), BF16),
            pltpu.VMEM((ch, 9 * chans), BF16),
            pltpu.VMEM((2 * lane_w, chans), BF16),
            pltpu.VMEM((lane_w, lane_w), BF16),
            pltpu.VMEM((degrees * ch, chans), BF16),
            pltpu.VMEM((2 * orders, width), BF16),
            pltpu.VMEM((2 * orders, width), BF16),
            pltpu.VMEM((rows, lane_w), F32),
            pltpu.VMEM((8, lat_total), F32),
            dma((5,)), dma((5,)), dma((2, np_)), dma((2, np_)), dma((np_,)), dma((np_,)), dma((8,)), pltpu.SemaphoreType.REGULAR,
        ],
        compiler_params=pltpu.CompilerParams(
            collective_id=0, has_side_effects=True, vmem_limit_bytes=60 << 20
        ),
    )(fields, w1, w2, mix, forward, inverse, quad, start)
    return out.reshape(ch, rows, width)


def solution(mesh):
    in_specs = (P("groups", "lat", "lon"), P(), P(), P(None, "lon", None))
    out_specs = P(("groups", "lon"), "lat", None)
    return jax.shard_map(
        functools.partial(local, mesh.shape["lat"]),
        mesh=mesh, in_specs=in_specs, out_specs=out_specs, check_vma=False,
    )
```

```python
import functools
import math

import jax
import jax.numpy as jnp
import numpy as np
from jax import lax
from jax.experimental import pallas as pl
from jax.experimental.pallas import tpu as pltpu
from jax.sharding import PartitionSpec as P

MESH = pl.DeviceIdType.MESH
BF16 = jnp.bfloat16
F32 = jnp.float32


def mm(a, b, dims=((1,), (0,))):
    return lax.dot_general(a, b, (dims, ((), ())), preferred_element_type=F32)


def constant_tables(lat_count, rows, lon_total, orders, width):
    lat_total = lat_count * rows
    per_x = 2 * orders // lat_count
    k = np.arange(lon_total)[:, None]
    m = np.arange(orders)[None, :]
    angle = (k * m % lon_total).astype(np.float64) * (2.0 * math.pi / lon_total)
    forward = np.stack([np.cos(angle), -np.sin(angle)], axis=-1).reshape(lon_total, 2 * orders)
    factor = np.where(np.arange(orders) == 0, 1.0, 2.0)[:, None, None]
    inverse = np.stack([np.cos(angle.T), -np.sin(angle.T)], axis=1) * factor
    inverse = inverse.reshape(2 * orders, lon_total)
    forward = forward.T.reshape(lat_count, per_x, lon_total).transpose(1, 0, 2)
    forward = forward.reshape(2 * orders, lon_total)
    theta = (np.arange(lat_total) + 0.5) * (math.pi / lat_total)
    quad = np.sin(theta) * (math.pi / lat_total / lon_total)
    quad = np.broadcast_to(quad.reshape(lat_count, rows, 1), (lat_count, rows, width))
    half = lat_total // 2
    fold = np.concatenate([np.arange(half), np.arange(half)[::-1]])
    cosine = np.cos(theta[fold])[None, :]
    counter = np.arange(1, orders + 1)
    sums = np.concatenate([[0.0], np.cumsum(np.log((2.0 * counter - 1.0) / (2.0 * counter)))])
    ids = np.arange(orders)
    start = (0.5 * np.log(ids + 0.5) + 0.5 * sums[ids])[:, None] + ids[:, None] * np.log(np.sin(theta[fold]))[None, :]
    start = start.reshape(lat_count, per_x // 2, lat_total)
    start = np.pad(start, ((0, 0), (0, 8 - per_x // 2), (0, 0)))
    start[:, 7] = cosine
    as_bf = lambda a: jnp.asarray(np.asarray(a, np.float32).astype(jnp.bfloat16))
    as_f = lambda a: jnp.asarray(np.ascontiguousarray(a, np.float32))
    return as_bf(forward), as_bf(inverse), as_f(quad), as_f(start)


def peers(np_, me):
    if np_ & (np_ - 1):
        return [lax.rem(me + d, np_) for d in range(np_ - 1, 0, -1)]
    out = []
    for d in range(np_ - 1, 0, -1):
        p, bit = me, 1
        while bit < np_:
            if d & bit:
                p = p + bit - 2 * bit * (me // bit % 2)
            bit *= 2
        out.append(p)
    return out


def body(sizes, x_hbm, w1_hbm, w2_hbm, mix_hbm, fwd_hbm, inv_hbm, quad_hbm, start_hbm, out_ref,
         xin, slab1, slab2, hdup, tb, send_b, recv_b, lt, lt_b, lg, spec, tc, send_c, recv_c, mixed,
         x_s, x32, x_ref, w1_ref, w2_ref, w1s, w2s, sq_s, sp_s, mix_s, fwd_s, inv_s, quad_s, start_s,
         a_send, a_recv, b_send, b_recv, c_send, c_recv, l_sem, ready):
    np_, rows, chans, half_w, degrees = sizes
    ch = chans // 2
    width = 2 * half_w
    per_x = 8
    orders_here = per_x // 2
    lat_total = np_ * rows
    lane_w = per_x * ch
    me = lax.axis_index("lat")
    core = lax.axis_index("lon")
    other = 1 - core

    barrier = pltpu.get_barrier_semaphore()

    others = peers(np_, me)

    def greet(p, h):
        pl.semaphore_signal(barrier, inc=1, device_id={"lat": p, "lon": h}, device_id_type=MESH)

    near = 1
    while near * near < np_ or np_ % near:
        near += 1
    far = np_ // near
    place = me % near
    far_others = [(me + near * d) % np_ for d in range(1, far)]
    crosses_up = (place == 0) & (me > 0)
    crosses_down = (place == near - 1) & (me < np_ - 1)
    for p in far_others:
        greet(p, core)

    @pl.when(crosses_up)
    def _():
        greet(me - 1, core)
        greet(me - 1, other)

    @pl.when(crosses_down)
    def _():
        greet(me + 1, core)
        greet(me + 1, other)

    for d in range(1, near):
        p = me - place + (place + d) % near
        greet(p, core)
        greet(p, other)
    greet(me, other)

    loads = [
        pltpu.make_async_copy(a, b, l_sem.at[k])
        for k, (a, b) in enumerate([
            (start_hbm.at[me], start_s), (quad_hbm.at[me], quad_s), (fwd_hbm, fwd_s),
            (mix_hbm, mix_s), (inv_hbm, inv_s), (x_hbm, x_s), (w1_hbm, w1_ref), (w2_hbm, w2_ref),
        ])
    ]
    for k in (5, 6, 7, 0, 1, 2, 3, 4):
        loads[k].start()

    for k in (5, 6, 7):
        loads[k].wait()
    for v in range(half_w // 128):
        x32[v] = x_s[:, :, v * 128 : (v + 1) * 128].astype(F32).reshape(chans * rows, 128)
        for t in range(rows):
            x_ref[t, :, v * 128 : (v + 1) * 128] = x32[v, pl.ds(t, chans, stride=rows), :].astype(BF16)
    for k in range(9):
        at = slice(k * chans, (k + 1) * chans)
        w1s[:, at] = w1_ref[k // 3, k % 3]
        w2s[:, at] = w2_ref[k // 3, k % 3, pl.ds(pl.multiple_of(core * ch, ch), ch), :]

    known = 2 * near - 1 + far - 1
    pl.semaphore_wait(
        barrier, known + 2 * crosses_up.astype(jnp.int32) + 2 * crosses_down.astype(jnp.int32)
    )

    def across():
        return pltpu.make_async_remote_copy(
            src_ref=x_ref, dst_ref=xin.at[core, pl.ds(2, rows)],
            send_sem=a_send.at[4], recv_sem=a_recv.at[4],
            device_id={"lat": me, "lon": other}, device_id_type=MESH,
        )

    def up(h):
        return pltpu.make_async_remote_copy(
            src_ref=x_ref.at[pl.ds(0, 2)], dst_ref=xin.at[core, pl.ds(rows + 2, 2)],
            send_sem=a_send.at[h], recv_sem=a_recv.at[h],
            device_id={"lat": jnp.maximum(me - 1, 0), "lon": (core + h) % 2}, device_id_type=MESH,
        )

    def down(h):
        return pltpu.make_async_remote_copy(
            src_ref=x_ref.at[pl.ds(rows - 2, 2)], dst_ref=xin.at[core, pl.ds(0, 2)],
            send_sem=a_send.at[2 + h], recv_sem=a_recv.at[2 + h],
            device_id={"lat": jnp.minimum(me + 1, np_ - 1), "lon": (core + h) % 2}, device_id_type=MESH,
        )

    @pl.when(me > 0)
    def _():
        up(0).start()
        up(1).start()

    @pl.when(me < np_ - 1)
    def _():
        down(0).start()
        down(1).start()

    across().start()

    for p in far_others:
        pl.semaphore_signal(ready, inc=1, device_id={"lat": p, "lon": core}, device_id_type=MESH)

    @pl.when(me == 0)
    def _():
        xin[:, pl.ds(0, 2)] = jnp.zeros((2, 2, chans, half_w), BF16)

    @pl.when(me == np_ - 1)
    def _():
        xin[:, pl.ds(rows + 2, 2)] = jnp.zeros((2, 2, chans, half_w), BF16)

    xin[core, pl.ds(2, rows)] = x_ref[...]

    loads[0].wait()
    cosine = start_s[7:8, :]
    log_start = start_s[...]
    wide_l = (8, degrees)
    order = (lax.broadcasted_iota(jnp.int32, wide_l, 0) + me * orders_here).astype(F32)
    degree = lax.broadcasted_iota(jnp.int32, wide_l, 1).astype(F32)
    earlier = degree - 1.0
    coef_a = jnp.sqrt(
        jnp.maximum(4.0 * degree * degree - 1.0, 1.0) / jnp.maximum(degree * degree - order * order, 1.0)
    )
    coef_b = coef_a * jnp.sqrt(
        jnp.maximum(earlier * earlier - order * order, 0.0) / jnp.maximum(4.0 * earlier * earlier - 1.0, 1.0)
    )
    wide_j = (8, lat_total)
    order_id = lax.broadcasted_iota(jnp.int32, wide_j, 0) + me * orders_here
    southern = lax.broadcasted_iota(jnp.int32, wide_j, 1) >= lat_total // 2
    sign_even = jnp.where(southern & (order_id % 2 == 1), -1.0, 1.0)
    sign_odd = jnp.where(southern & (order_id % 2 == 0), -1.0, 1.0)
    start_scale = jnp.exp(log_start)
    span = 32 if degrees % 32 == 0 else degrees
    current = previous = log_scale = scale = jnp.zeros(wide_j, F32)
    for l_id in range(degrees):
        is_start = order_id == l_id
        newest = (
            (coef_a[:, l_id : l_id + 1] * cosine) * current
            - coef_b[:, l_id : l_id + 1] * previous
            + jnp.where(is_start, 1.0, 0.0)
        )
        scale = jnp.where(is_start, start_scale, scale)
        previous, current = current, newest
        value = newest * (scale * (sign_odd if l_id % 2 else sign_even))
        for v in range(lat_total // 128):
            lt[v, l_id * 8 : (l_id + 1) * 8, :] = value[:, v * 128 : (v + 1) * 128]
        if (l_id + 1) % span == 0 and l_id + 1 < degrees:
            log_scale = jnp.where((order_id > l_id - span) & (order_id <= l_id), log_start, log_scale)
            size_now = jnp.maximum(jnp.abs(current), jnp.abs(previous))
            safe = jnp.where(size_now > 0.0, size_now, 1.0)
            current = current / safe
            previous = previous / safe
            log_scale = log_scale + jnp.log(safe)
            scale = jnp.exp(log_scale)
    across().wait()

    def fill(slab, t, wide):
        base = t * 3 * chans
        slab[base : base + chans, :] = pltpu.roll(wide, 1, 1).astype(BF16)
        slab[base + chans : base + 2 * chans, :] = wide.astype(BF16)
        slab[base + 2 * chans : base + 3 * chans, :] = pltpu.roll(wide, width - 1, 1).astype(BF16)

    def row_in(t):
        return jnp.concatenate([xin[0, t].astype(F32), xin[1, t].astype(F32)], axis=1)

    for t in range(2, rows + 2):
        fill(slab1, t, row_in(t))

    @pl.when(me > 0)
    def _():
        up(0).wait_send()
        up(1).wait_send()
        down(0).wait_recv()
        down(1).wait_recv()

    @pl.when(me < np_ - 1)
    def _():
        down(0).wait_send()
        down(1).wait_send()
        up(0).wait_recv()
        up(1).wait_recv()

    for t in (0, 1, rows + 2, rows + 3):
        fill(slab1, t, row_in(t))

    w1 = w1s[...]
    w2 = w2s[...]
    depth = 9 * chans
    for t in range(rows + 2):
        first = mm(w1, slab1[t * 3 * chans : t * 3 * chans + depth, :])
        first = jnp.maximum(first, 0.0)
        if t == 0:
            first = jnp.where(me > 0, first, 0.0)
        if t == rows + 1:
            first = jnp.where(me < np_ - 1, first, 0.0)
        fill(slab2, t, first)

    dup = 128 // ch
    for t in range(rows):
        second = mm(w2, slab2[t * 3 * chans : t * 3 * chans + depth, :])
        second = jnp.maximum(second, 0.0).astype(BF16)
        for g in range(dup):
            hdup[t * 128 + g * ch : t * 128 + (g + 1) * ch, :] = second

    loads[1].wait()
    loads[2].wait()
    fwd = fwd_s[...]
    group = lax.broadcasted_iota(jnp.int32, (np_, 128), 1) // ch
    for j in range(rows):
        s = mm(fwd, hdup[j * 128 : (j + 1) * 128, :], ((1,), (1,)))
        for xh in range(lane_w // 128):
            acc = s[xh * dup * np_ : (xh * dup + 1) * np_, :]
            for g in range(1, dup):
                at = (xh * dup + g) * np_
                acc = jnp.where(group == g, s[at : at + np_, :], acc)
            tb[xh, pl.ds(j, np_, stride=rows), :] = acc
    quad = quad_s[...]
    for p in range(np_):
        piece = jnp.concatenate(
            [tb[xh, p * rows : (p + 1) * rows, :] for xh in range(lane_w // 128)], axis=1
        )
        send_b[p] = (piece * quad).astype(BF16)

    pl.semaphore_wait(ready, far - 1)

    def b_copy(to_lat, to_core, from_lat, from_core):
        return pltpu.make_async_remote_copy(
            src_ref=send_b.at[to_lat], dst_ref=recv_b.at[from_core, from_lat],
            send_sem=b_send.at[to_core, to_lat], recv_sem=b_recv.at[from_core, from_lat],
            device_id={"lat": to_lat, "lon": to_core}, device_id_type=MESH,
        )

    for p in others:
        b_copy(p, core, me, core).start()
    recv_b[core, me] = send_b[me]

    for q in range(orders_here):
        table = jnp.concatenate(
            [lt[v, pl.ds(q, degrees, stride=8), :] for v in range(lat_total // 128)], axis=1
        )
        lt_b[q * degrees : (q + 1) * degrees, :] = table.astype(BF16)
        lg[q] = table.T.astype(BF16)
    at = lax.broadcasted_iota(jnp.int32, (2 * lane_w, chans), 0)
    place = at // lane_w * ch + at % ch
    sq_s[...] = jnp.where(
        place == lax.broadcasted_iota(jnp.int32, (2 * lane_w, chans), 1), 1.0, 0.0
    ).astype(BF16)
    sp_s[...] = jnp.where(
        lax.broadcasted_iota(jnp.int32, (lane_w, rows * ch), 0) % ch
        == lax.broadcasted_iota(jnp.int32, (lane_w, rows * ch), 1) // rows, 1.0, 0.0
    ).astype(BF16)
    pick = jnp.where(
        lax.broadcasted_iota(jnp.int32, (np_, lat_total), 0)
        == lax.broadcasted_iota(jnp.int32, (np_, lat_total), 1) // rows, 1.0, 0.0
    ).astype(BF16)
    loads[3].wait()
    loads[4].wait()

    def pass_on(h):
        return pltpu.make_async_remote_copy(
            src_ref=recv_b.at[h], dst_ref=recv_b.at[h],
            send_sem=b_send.at[other, 0], recv_sem=b_recv.at[h, 0],
            device_id={"lat": me, "lon": other}, device_id_type=MESH,
        )

    for q in reversed(others):
        b_copy(q, core, q, core).wait_recv()
    pass_on(core).start()

    table = lt_b[...]
    x_lane = lax.broadcasted_iota(jnp.int32, (degrees, lane_w), 1) // ch
    def half(h):
        return mm(table, recv_b[h].astype(F32).reshape(lat_total, lane_w).astype(BF16))

    mine = half(core)
    pass_on(other).wait_recv()
    theirs = half(other)
    halves = [jnp.where(core == 0, mine, theirs), jnp.where(core == 0, theirs, mine)]
    for x in range(per_x):
        q = x // 2
        part = [jnp.where(x_lane == x, u[q * degrees : (q + 1) * degrees, :], 0.0).astype(BF16) for u in halves]
        spec[x * degrees : (x + 1) * degrees, :] = mm(jnp.concatenate(part, axis=1), sq_s[...])

    sub = 8
    block = per_x * sub
    own = (
        lax.broadcasted_iota(jnp.int32, (block, sub * ch), 0) % sub
        == lax.broadcasted_iota(jnp.int32, (block, sub * ch), 1) // ch
    )
    for s in range(degrees // sub):
        lhs = jnp.concatenate(
            [spec[x * degrees + s * sub : x * degrees + (s + 1) * sub, :] for x in range(per_x)], axis=0
        ).astype(BF16)
        rhs = mix_s[s * sub * ch : (s + 1) * sub * ch, :]
        both = jnp.where(own, mm(lhs, rhs, ((1,), (1,))), 0.0).astype(BF16)
        wide = mm(both, sp_s[...])
        for x in range(per_x):
            mixed[x * degrees + s * sub : x * degrees + (s + 1) * sub, :] = wide[x * sub : (x + 1) * sub, :]

    own_row = (
        lax.broadcasted_iota(jnp.int32, (lat_total, lane_w), 0) % rows
        == lax.broadcasted_iota(jnp.int32, (lat_total, lane_w), 1) % rows
    )
    for x in range(per_x):
        y = mm(lg[x // 2], mixed[x * degrees : (x + 1) * degrees, :].astype(BF16))
        y = jnp.where(own_row, y, 0.0).astype(BF16)
        z = mm(pick, y)
        for xh in range(lane_w // 128):
            tc[xh, pl.ds(x, np_, stride=per_x), :] = z[:, xh * 128 : (xh + 1) * 128]
    for p in range(np_):
        send_c[p] = jnp.concatenate(
            [tc[xh, p * per_x : (p + 1) * per_x, :] for xh in range(lane_w // 128)], axis=1
        ).astype(BF16)

    def c_copy(to_lat, from_lat):
        return pltpu.make_async_remote_copy(
            src_ref=send_c.at[to_lat], dst_ref=recv_c.at[from_lat],
            send_sem=c_send.at[to_lat], recv_sem=c_recv.at[from_lat],
            device_id={"lat": to_lat, "lon": core}, device_id_type=MESH,
        )

    for p in others:
        c_copy(p, me).start()
    recv_c[me] = send_c[me]

    pass_on(core).wait_send()
    for p in others:
        b_copy(p, core, me, core).wait_send()

    for q in reversed(others):
        c_copy(q, q).wait_recv()
    full = recv_c[...].astype(F32).reshape(np_ * per_x, lane_w).T.astype(BF16)
    out_ref[...] = mm(full, inv_s[...]).astype(BF16)
    for p in others:
        c_copy(p, me).wait_send()


def local(np_, fields, conv_first, conv_second, mixing):
    chans, rows, half_w = fields.shape
    ch = chans // 2
    width = 2 * half_w
    lat_total = np_ * rows
    orders = lat_total // 2
    degrees = mixing.shape[0]
    per_x = 2 * orders // np_
    lane_w = per_x * ch
    forward, inverse, quad, start = constant_tables(np_, rows, width, orders, lane_w)
    w1 = jnp.transpose(conv_first, (2, 3, 0, 1))
    w2 = jnp.transpose(conv_second, (2, 3, 0, 1))
    mix = mixing.reshape(degrees * ch, chans)
    vm = pl.BlockSpec(memory_space=pltpu.VMEM)
    hbm = pl.BlockSpec(memory_space=pl.ANY)
    dma = pltpu.SemaphoreType.DMA
    out = pl.pallas_call(
        functools.partial(body, (np_, rows, chans, half_w, degrees)),
        out_shape=jax.ShapeDtypeStruct((ch * rows, width), BF16),
        in_specs=[hbm] * 8,
        out_specs=vm,
        scratch_shapes=[
            pltpu.VMEM((2, rows + 4, chans, half_w), BF16),
            pltpu.VMEM(((rows + 4) * 3 * chans, width), BF16),
            pltpu.VMEM(((rows + 2) * 3 * chans, width), BF16),
            pltpu.VMEM((rows * 128, width), BF16),
            pltpu.VMEM((lane_w // 128, lat_total, 128), F32),
            pltpu.VMEM((np_, rows, lane_w), BF16),
            pltpu.VMEM((2, np_, rows, lane_w), BF16),
            pltpu.VMEM((lat_total // 128, 8 * degrees, 128), F32),
            pltpu.VMEM((per_x // 2 * degrees, lat_total), BF16),
            pltpu.VMEM((per_x // 2, lat_total, degrees), BF16),
            pltpu.VMEM((per_x * degrees, chans), F32),
            pltpu.VMEM((lane_w // 128, np_ * per_x, 128), F32),
            pltpu.VMEM((np_, per_x, lane_w), BF16),
            pltpu.VMEM((np_, per_x, lane_w), BF16),
            pltpu.VMEM((per_x * degrees, lane_w), F32),
            pltpu.VMEM((chans, rows, half_w), BF16),
            pltpu.VMEM((half_w // 128, chans * rows, 128), F32),
            pltpu.VMEM((rows, chans, half_w), BF16),
            pltpu.VMEM((3, 3, chans, chans), BF16),
            pltpu.VMEM((3, 3, chans, chans), BF16),
            pltpu.VMEM((chans, 9 * chans), BF16),
            pltpu.VMEM((ch, 9 * chans), BF16),
            pltpu.VMEM((2 * lane_w, chans), BF16),
            pltpu.VMEM((lane_w, lane_w), BF16),
            pltpu.VMEM((degrees * ch, chans), BF16),
            pltpu.VMEM((2 * orders, width), BF16),
            pltpu.VMEM((2 * orders, width), BF16),
            pltpu.VMEM((rows, lane_w), F32),
            pltpu.VMEM((8, lat_total), F32),
            dma((5,)), dma((5,)), dma((2, np_)), dma((2, np_)), dma((np_,)), dma((np_,)), dma((8,)), pltpu.SemaphoreType.REGULAR,
        ],
        compiler_params=pltpu.CompilerParams(
            collective_id=0, has_side_effects=True, vmem_limit_bytes=60 << 20
        ),
    )(fields, w1, w2, mix, forward, inverse, quad, start)
    return out.reshape(ch, rows, width)


def solution(mesh):
    in_specs = (P("groups", "lat", "lon"), P(), P(), P(None, "lon", None))
    out_specs = P(("groups", "lon"), "lat", None)
    return jax.shard_map(
        functools.partial(local, mesh.shape["lat"]),
        mesh=mesh, in_specs=in_specs, out_specs=out_specs, check_vma=False,
    )
```
